32 devices in a mesh: groups: 2 (over y), tile: 4 (over z), chan: 4 (over x, core).
Axes of the slice: x: 2, y: 2, z: 4, core: 2. Of those that a mesh axis runs over, the one named last changes fastest.
Arguments:
- tokens: bfloat16 [1024, 384], P(('groups', 'tile'), 'chan'), parts along dimension 0, may hold values from -6 to 6
- conv_a: bfloat16 [27, 384, 384], P(None, 'chan'), may hold values from -0.0625 to 0.0625
- bias_a: float32 [384], P('chan'), may hold values from -3 to 3
- conv_b: bfloat16 [27, 384, 384], P(None, 'chan'), may hold values from -0.0625 to 0.0625
- bias_b: float32 [384], P('chan'), may hold values from -3 to 3
Outputs:
- decoded: bfloat16 [384, 16, 256], P('chan', 'tile', 'groups'), parts along dimension 2
The draws below stay inside these ranges and needn't reach their ends.
There are 2 independent parts, one for each index of `groups`. The reference program is written for one: setup_inputs(seed, part) draws one part's arguments, and reference() takes and returns one part's arrays. A program takes and returns all parts, laid end to end along the dimension named above; an argument that names none is the same for every part. Nothing has to cross between parts.
All inputs are finite; a program needn't handle non-finite values.
Results may differ from the reference program's by a relative error of at most 0.0038.
Values may be sent and summed in bfloat16 or wider, within the bound.
A program may use at most 64 MiB of HBM per device.

```python
import jax
import jax.numpy as jnp
from jax import lax

C = 384
TF = 4
H = 16
W = 8
S = 512
H2 = 32
W2 = 16


def block_levels(rng, extent, pieces, smallest, high):
    loudness, own = 1.0, jax.random.fold_in(rng, 6)
    for position, parts in pieces:
        heights = jnp.exp(jax.random.uniform(jax.random.fold_in(own, position), (parts,), jnp.float32, smallest / len(pieces), high / len(pieces)))
        loudness = loudness * jnp.repeat(heights, extent[position] // parts).reshape([-1 if axis == position else 1 for axis in range(len(extent))])
    return loudness


def gaussian(key, extent, spread, most, split=(), held_as=jnp.bfloat16):
    values = jax.random.normal(key, extent, jnp.float32) * spread
    if len(split) > 0:
        values = block_levels(key, extent, split, -0.22, 0.18) * values
    return jnp.clip(values, min=-most, max=most).astype(held_as)


def setup_inputs(seed: int = 0, part: int = 0) -> dict:
    streams_of = jax.random.split(jax.random.key(seed), 6)
    part_splits = jax.random.split(jax.random.fold_in(streams_of[5], part), 6)
    tokens = gaussian(part_splits[0], (S, C), 1.0, 6.0, ((0, 4), (1, 4)))
    conv_a = gaussian(streams_of[1], (27, C, C), (27 * C) ** -0.5, 0.0625, ((1, 4),))
    bias_a = gaussian(streams_of[2], (C,), 0.5, 3.0, ((0, 4),), jnp.float32)
    conv_b = gaussian(streams_of[3], (27, C, C), (27 * C) ** -0.5, 0.0625, ((1, 4),))
    bias_b = gaussian(streams_of[4], (C,), 0.5, 3.0, ((0, 4),), jnp.float32)
    return {"tokens": tokens, "conv_a": conv_a, "bias_a": bias_a, "conv_b": conv_b, "bias_b": bias_b}


def causal_conv(field, weight, bias):
    padded = jnp.pad(field.astype(jnp.float32), ((0, 0), (2, 0), (1, 1), (1, 1)))
    kernel = weight.astype(jnp.float32).reshape(3, 3, 3, C, C).transpose(4, 3, 0, 1, 2)
    result = lax.conv_general_dilated(padded[None], kernel, (1, 1, 1), "VALID",
                                      dimension_numbers=("NCDHW", "OIDHW", "NCDHW"),
                                      precision=lax.Precision.HIGHEST)[0]
    return jax.nn.silu(result + bias.astype(jnp.float32)[:, None, None, None])


def reference(tokens, conv_a, bias_a, conv_b, bias_b):
    field = tokens.reshape(TF, H, W, C).transpose(3, 0, 1, 2)
    first = causal_conv(field, conv_a, bias_a).astype(jnp.bfloat16)
    upsampled = jnp.repeat(jnp.repeat(first, 2, axis=2), 2, axis=3)
    second = causal_conv(upsampled, conv_b, bias_b).astype(jnp.bfloat16)
    return second.transpose(0, 3, 1, 2).reshape(C, W2, TF * H2)
```

```python
import functools

import jax
import jax.numpy as jnp
from jax import lax
from jax.experimental import pallas as pl
from jax.experimental.pallas import tpu as pltpu
from jax.sharding import PartitionSpec as P

TF = 4
H = 16
H2 = 2 * H
WD = 2
LANES = 128
POS = WD * TF * H
COL = TF * H2
MESH = pl.DeviceIdType.MESH
CHUNKS = ((1, 2), (0, 3))


def silu(v):
    return v / (1.0 + jnp.exp(-v))


def kernel(tiles, chans, ch, rows,
           tok_hbm, wa_hbm, ba_hbm, wb_hbm, bb_hbm, out_ref,
           tok, tokf, fsend, frecv, fpad, xs, wa, wb, ba, bb, bias_a,
           asend, arecv, hsend, hrecv, gpad, us, bsend, brecv,
           lsem, fs_sem, fr_sem, as_sem, ar_sem, hs_sem, hr_sem, bs_sem, br_sem):
    mt = lax.axis_index("tile")
    mc = lax.axis_index("chan")
    width = tiles * WD
    f32, bf16 = jnp.float32, jnp.bfloat16

    tok_copy = pltpu.make_async_copy(tok_hbm, tok, lsem.at[0])
    tok_copy.start()
    wa_copy = pltpu.make_async_copy(wa_hbm, wa.at[:, pl.ds(0, ch), :], lsem.at[1])
    wa_copy.start()
    ba_copy = pltpu.make_async_copy(ba_hbm, ba, lsem.at[2])
    ba_copy.start()
    bb_copy = pltpu.make_async_copy(bb_hbm, bb, lsem.at[3])
    bb_copy.start()
    wb_copy = pltpu.make_async_copy(wb_hbm, wb.at[:, pl.ds(0, ch), :], lsem.at[4])
    wb_copy.start()

    hrecv[...] = jnp.zeros_like(hrecv)
    barrier = pltpu.get_barrier_semaphore()
    for k in range(1, tiles):
        pl.semaphore_signal(barrier, inc=1, device_id={"tile": lax.rem(mt + k, tiles)}, device_id_type=MESH)
    for k in range(1, chans):
        pl.semaphore_signal(barrier, inc=1, device_id={"chan": lax.rem(mc + k, chans)}, device_id_type=MESH)

    tokf[...] = jnp.zeros_like(tokf)
    fsend[0] = jnp.zeros_like(fsend[0])
    fsend[width + 1] = jnp.zeros_like(fsend[0])
    tok_copy.wait()
    tokf[:, :ch] = tok[...].astype(f32)
    for w in range(width):
        fsend[w + 1] = tokf[pl.ds(w, rows, stride=width), :].astype(bf16)

    pl.semaphore_wait(barrier, tiles + chans - 2)

    def field_copy(k, src_tile, peer):
        return pltpu.make_async_remote_copy(
            src_ref=fsend.at[pl.ds(WD * peer, WD + 2)], dst_ref=frecv.at[src_tile],
            send_sem=fs_sem.at[k - 1], recv_sem=fr_sem.at[k - 1],
            device_id={"tile": peer}, device_id_type=MESH)

    for k in range(1, tiles):
        field_copy(k, mt, lax.rem(mt + k, tiles)).start()
    frecv[mt] = fsend[pl.ds(WD * mt, WD + 2)]

    wa[:, ch:, :] = jnp.zeros((27, LANES - ch, wa.shape[2]), bf16)
    wb[:, ch:, :] = jnp.zeros((27, LANES - ch, wb.shape[2]), bf16)
    fpad[:, :, 0:8, :] = jnp.zeros((WD + 2, TF, 8, LANES), f32)
    fpad[:, :, 8 + H:16 + H, :] = jnp.zeros((WD + 2, TF, 8, LANES), f32)
    gpad[:, :, 0:8, :] = jnp.zeros((WD + 2, TF, 8, LANES), f32)
    gpad[:, :, 8 + H2:16 + H2, :] = jnp.zeros((WD + 2, TF, 8, LANES), f32)
    xs[:, :, 0:2] = jnp.zeros((3, WD + 2, 2, H, LANES), bf16)
    us[:, :, 0:2] = jnp.zeros((3, WD + 2, 2, H2, LANES), bf16)
    asend[...] = jnp.zeros_like(asend)
    bias_a[...] = jnp.zeros_like(bias_a)
    ba_copy.wait()
    bias_a[:, :ch] = ba[...]

    for k in range(1, tiles):
        field_copy(k, lax.rem(mt + tiles - k, tiles), lax.rem(mt + k, tiles)).wait_recv()

    for s in range(tiles):
        t, h0 = (s * rows) // H, (s * rows) % H
        fpad[:, t, 8 + h0:8 + h0 + rows, :] = frecv[s].astype(f32)
    for e in range(3):
        xs[e, :, 2:] = fpad[:, :, 7 + e:7 + e + H, :].astype(bf16)

    wa_copy.wait()
    lhs = jnp.concatenate(
        [xs[e, g:g + WD, a:a + TF].reshape(POS, LANES)
         for a in range(3) for e in range(3) for g in range(3)], axis=1)
    part = jnp.dot(lhs, wa[...].reshape(27 * LANES, wa.shape[2]), preferred_element_type=f32)
    for j in range(chans):
        asend[j, :, :ch] = part[:, j * ch:(j + 1) * ch]

    def a_copy(k):
        peer = lax.rem(mc + k, chans)
        return pltpu.make_async_remote_copy(
            src_ref=asend.at[peer], dst_ref=arecv.at[k - 1],
            send_sem=as_sem.at[k - 1], recv_sem=ar_sem.at[k - 1],
            device_id={"chan": peer}, device_id_type=MESH)

    for k in range(1, chans):
        a_copy(k).start()
    total = asend[mc] + bias_a[...]
    for k in range(1, chans):
        a_copy(k).wait_recv()
        total = total + arecv[k - 1]
    first = silu(total).astype(bf16).reshape(WD, TF, H, LANES)

    hsend[0] = first[0]
    hsend[1] = first[WD - 1]

    def halo_copy(side, peer):
        return pltpu.make_async_remote_copy(
            src_ref=hsend.at[side], dst_ref=hrecv.at[1 - side],
            send_sem=hs_sem.at[side], recv_sem=hr_sem.at[1 - side],
            device_id={"tile": peer}, device_id_type=MESH)

    has_left = mt > 0
    has_right = mt < tiles - 1

    @pl.when(has_left)
    def _():
        halo_copy(0, mt - 1).start()

    @pl.when(has_right)
    def _():
        halo_copy(1, mt + 1).start()

    def place(w, column):
        column = column.astype(f32)
        for t in range(TF):
            for parity in range(2):
                gpad.at[w, t][pl.ds(8 + parity, H, stride=2), :] = column[t]
        for e in range(3):
            us[e, w, 2:] = gpad[w, :, 7 + e:7 + e + H2, :].astype(bf16)

    for w in range(WD):
        place(w + 1, first[w])

    def b_copy(c, k):
        peer = lax.rem(mc + k, chans)
        return pltpu.make_async_remote_copy(
            src_ref=bsend.at[c, peer], dst_ref=brecv.at[c, k - 1],
            send_sem=bs_sem.at[c, k - 1], recv_sem=br_sem.at[c, k - 1],
            device_id={"chan": peer}, device_id_type=MESH)

    wb_copy.wait()
    bb_copy.wait()
    for c, cols in enumerate(CHUNKS):
        if c == 1:
            @pl.when(has_right)
            def _():
                halo_copy(0, mt).wait_recv()

            @pl.when(has_left)
            def _():
                halo_copy(1, mt).wait_recv()
            place(0, hrecv[0])
            place(WD + 1, hrecv[1])
        lhs = jnp.concatenate(
            [jnp.concatenate(
                [us[e, (w2 + g + 1) // 2, a:a + TF].reshape(COL, LANES) for w2 in cols], axis=0)
             for a in range(3) for e in range(3) for g in range(3)], axis=1)
        part = jnp.dot(lhs, wb[...].reshape(27 * LANES, wb.shape[2]), preferred_element_type=f32)
        for j in range(chans):
            bsend[c, j] = part[:, j * ch:(j + 1) * ch].astype(bf16)
        for k in range(1, chans):
            b_copy(c, k).start()

    for c, cols in enumerate(CHUNKS):
        total = bsend[c, mc].astype(f32) + bb[...]
        for k in range(1, chans):
            b_copy(c, k).wait_recv()
            total = total + brecv[c, k - 1].astype(f32)
        y = silu(total)
        for i, w2 in enumerate(cols):
            out_ref[w2] = y[i * COL:(i + 1) * COL].T.astype(bf16)

    for k in range(1, tiles):
        field_copy(k, mt, lax.rem(mt + k, tiles)).wait_send()
    for k in range(1, chans):
        a_copy(k).wait_send()
        for c in range(2):
            b_copy(c, k).wait_send()

    @pl.when(has_left)
    def _():
        halo_copy(0, mt - 1).wait_send()

    @pl.when(has_right)
    def _():
        halo_copy(1, mt + 1).wait_send()


def local(tokens, conv_a, bias_a, conv_b, bias_b):
    tiles = lax.axis_size("tile")
    chans = lax.axis_size("chan")
    ch = tokens.shape[1]
    rows = TF * H // tiles
    full = conv_a.shape[2]
    width = tiles * WD
    f32, bf16 = jnp.float32, jnp.bfloat16
    vm, dma = pltpu.VMEM, pltpu.SemaphoreType.DMA
    out = pl.pallas_call(
        functools.partial(kernel, tiles, chans, ch, rows),
        out_shape=jax.ShapeDtypeStruct((2 * WD, ch, COL), bf16),
        in_specs=[pl.BlockSpec(memory_space=pl.ANY)] * 5,
        out_specs=pl.BlockSpec(memory_space=vm),
        scratch_shapes=[
            vm((rows * width, ch), bf16),
            vm((rows * width, LANES), f32),
            vm((width + 2, rows, LANES), bf16),
            vm((tiles, WD + 2, rows, LANES), bf16),
            vm((WD + 2, TF, H + 16, LANES), f32),
            vm((3, WD + 2, TF + 2, H, LANES), bf16),
            vm((27, LANES, full), bf16),
            vm((27, LANES, full), bf16),
            vm((1, ch), f32),
            vm((1, ch), f32),
            vm((1, LANES), f32),
            vm((chans, POS, LANES), f32),
            vm((chans - 1, POS, LANES), f32),
            vm((2, TF, H, LANES), bf16),
            vm((2, TF, H, LANES), bf16),
            vm((WD + 2, TF, H2 + 16, LANES), f32),
            vm((3, WD + 2, TF + 2, H2, LANES), bf16),
            vm((2, chans, 2 * COL, ch), bf16),
            vm((2, chans - 1, 2 * COL, ch), bf16),
            dma((5,)),
            dma((tiles - 1,)),
            dma((tiles - 1,)),
            dma((chans - 1,)),
            dma((chans - 1,)),
            dma((2,)),
            dma((2,)),
            dma((2, chans - 1)),
            dma((2, chans - 1)),
        ],
        compiler_params=pltpu.CompilerParams(
            collective_id=0, has_side_effects=True, vmem_limit_bytes=48 << 20),
    )(tokens, conv_a, bias_a.reshape(1, -1), conv_b, bias_b.reshape(1, -1))
    return out.transpose(1, 0, 2)


def solution(mesh):
    in_specs = (
        P(("groups", "tile"), "chan"),
        P(None, "chan", None),
        P("chan"),
        P(None, "chan", None),
        P("chan"),
    )
    out_specs = P("chan", "tile", "groups")
    return jax.shard_map(local, mesh=mesh, in_specs=in_specs, out_specs=out_specs, check_vma=False)
```

```python
import functools

import jax
import jax.numpy as jnp
from jax import lax
from jax.experimental import pallas as pl
from jax.experimental.pallas import tpu as pltpu
from jax.sharding import PartitionSpec as P

TF = 4
H = 16
H2 = 2 * H
WD = 2
LANES = 128
POS = WD * TF * H
COL = TF * H2
MESH = pl.DeviceIdType.MESH
CHUNKS = ((1, 2), (0, 3))


def silu(v):
    return v / (1.0 + jnp.exp(-v))


def kernel(tiles, chans, ch, rows,
           tok_hbm, wa_hbm, ba_hbm, wb_hbm, bb_hbm, out_ref,
           tok, tokf, fsend, frecv, fpad, xs, wa, wb, ba, bb, bias_a,
           bias_b, asend, a_near, a_pass, a_far, hsend, hrecv, gpad, us, bsend, b_near, b_pass, b_far,
           lsem, fs_sem, fr_sem, an_sem, am_sem, ap_sem, af_sem, hs_sem, hr_sem,
           bn_sem, bm_sem, bp_sem, bf_sem):
    mt = lax.axis_index("tile")
    mc = lax.axis_index("chan")
    width = tiles * WD
    f32, bf16 = jnp.float32, jnp.bfloat16
    pairs = chans // 2
    side, pair = lax.rem(mc, 2), mc // 2
    partner = mc + 1 - 2 * side

    tok_copy = pltpu.make_async_copy(tok_hbm, tok, lsem.at[0])
    tok_copy.start()
    wa_copy = pltpu.make_async_copy(wa_hbm, wa.at[:, pl.ds(0, ch), :], lsem.at[1])
    wa_copy.start()
    ba_copy = pltpu.make_async_copy(ba_hbm, ba, lsem.at[2])
    ba_copy.start()
    bb_copy = pltpu.make_async_copy(bb_hbm, bb, lsem.at[3])
    bb_copy.start()
    wb_copy = pltpu.make_async_copy(wb_hbm, wb.at[:, pl.ds(0, ch), :], lsem.at[4])
    wb_copy.start()

    hrecv[...] = jnp.zeros_like(hrecv)
    barrier = pltpu.get_barrier_semaphore()
    for k in range(1, tiles):
        pl.semaphore_signal(barrier, inc=1, device_id={"tile": lax.rem(mt + k, tiles)}, device_id_type=MESH)
    pl.semaphore_signal(barrier, inc=1, device_id={"chan": partner}, device_id_type=MESH)
    for k in range(1, pairs):
        pl.semaphore_signal(
            barrier, inc=1, device_id={"chan": 2 * lax.rem(pair + k, pairs) + side}, device_id_type=MESH)

    tokf[...] = jnp.zeros_like(tokf)
    fsend[0] = jnp.zeros_like(fsend[0])
    fsend[width + 1] = jnp.zeros_like(fsend[0])
    tok_copy.wait()
    tokf[:, :ch] = tok[...].astype(f32).T
    for w in range(width):
        fsend[w + 1] = tokf[pl.ds(w, rows, stride=width), :].astype(bf16)

    pl.semaphore_wait(barrier, tiles - 1 + pairs)

    def field_copy(k, src_tile, peer):
        return pltpu.make_async_remote_copy(
            src_ref=fsend.at[pl.ds(WD * peer, WD + 2)], dst_ref=frecv.at[src_tile],
            send_sem=fs_sem.at[k - 1], recv_sem=fr_sem.at[k - 1],
            device_id={"tile": peer}, device_id_type=MESH)

    for k in range(1, tiles):
        field_copy(k, mt, lax.rem(mt + k, tiles)).start()
    frecv[mt] = fsend[pl.ds(WD * mt, WD + 2)]

    wa[:, ch:, :] = jnp.zeros((27, LANES - ch, wa.shape[2]), bf16)
    wb[:, ch:, :] = jnp.zeros((27, LANES - ch, wb.shape[2]), bf16)
    fpad[:, :, 0:8, :] = jnp.zeros((WD + 2, TF, 8, LANES), f32)
    fpad[:, :, 8 + H:16 + H, :] = jnp.zeros((WD + 2, TF, 8, LANES), f32)
    gpad[:, :, 0:8, :] = jnp.zeros((WD + 2, TF, 8, LANES), f32)
    gpad[:, :, 8 + H2:16 + H2, :] = jnp.zeros((WD + 2, TF, 8, LANES), f32)
    xs[:, :, 0:2] = jnp.zeros((3, WD + 2, 2, H, LANES), bf16)
    us[:, :, 0:2] = jnp.zeros((3, WD + 2, 2, H2, LANES), bf16)
    ba_copy.wait()
    bb_copy.wait()
    for row, column in ((ba, bias_a), (bb, bias_b)):
        wide = jnp.concatenate([row[...], jnp.zeros((1, LANES - ch), f32)], axis=1)
        column[...] = jnp.broadcast_to(wide, (LANES, LANES)).T[:ch]

    for k in range(1, tiles):
        field_copy(k, lax.rem(mt + tiles - k, tiles), lax.rem(mt + k, tiles)).wait_recv()

    for s in range(tiles):
        t, h0 = (s * rows) // H, (s * rows) % H
        fpad[:, t, 8 + h0:8 + h0 + rows, :] = frecv[s].astype(f32)
    for e in range(3):
        xs[e, :, 2:] = fpad[:, :, 7 + e:7 + e + H, :].astype(bf16)

    wa_copy.wait()
    lhs = jnp.concatenate(
        [xs[e, g:g + WD, a:a + TF].reshape(POS, LANES)
         for a in range(3) for e in range(3) for g in range(3)], axis=1)
    part = jnp.dot(lhs, wa[...].reshape(27 * LANES, wa.shape[2]), preferred_element_type=f32)
    part = part.T
    for j in range(chans):
        asend[j] = part[j * ch:(j + 1) * ch]

    def near_copy(k, send, near, send_sem, recv_sem):
        return pltpu.make_async_remote_copy(
            src_ref=send.at[2 * lax.rem(pair + k, pairs) + 1 - side], dst_ref=near.at[k],
            send_sem=send_sem.at[k], recv_sem=recv_sem.at[k],
            device_id={"chan": partner}, device_id_type=MESH)

    def far_copy(k, held, far, send_sem, recv_sem):
        return pltpu.make_async_remote_copy(
            src_ref=held.at[k - 1], dst_ref=far.at[k - 1],
            send_sem=send_sem.at[k - 1], recv_sem=recv_sem.at[k - 1],
            device_id={"chan": 2 * lax.rem(pair + k, pairs) + side}, device_id_type=MESH)

    order = [*range(1, pairs), 0]
    a_near_args = (asend, a_near, an_sem, am_sem)
    a_far_args = (a_pass, a_far, ap_sem, af_sem)
    for k in order:
        near_copy(k, *a_near_args).start()
    for k in range(1, pairs):
        near_copy(k, *a_near_args).wait_recv()
        a_pass[k - 1] = asend[2 * lax.rem(pair + k, pairs) + side] + a_near[k]
        far_copy(k, *a_far_args).start()
    near_copy(0, *a_near_args).wait_recv()
    total = asend[mc] + a_near[0] + bias_a[...]
    for k in range(1, pairs):
        far_copy(k, *a_far_args).wait_recv()
        total = total + a_far[k - 1]
    first = jnp.concatenate([silu(total), jnp.zeros((LANES - ch, POS), f32)], axis=0).T
    first = first.astype(bf16).reshape(WD, TF, H, LANES)

    hsend[0] = first[0]
    hsend[1] = first[WD - 1]

    def halo_copy(side, peer):
        return pltpu.make_async_remote_copy(
            src_ref=hsend.at[side], dst_ref=hrecv.at[1 - side],
            send_sem=hs_sem.at[side], recv_sem=hr_sem.at[1 - side],
            device_id={"tile": peer}, device_id_type=MESH)

    has_left = mt > 0
    has_right = mt < tiles - 1

    @pl.when(has_left)
    def _():
        halo_copy(0, mt - 1).start()

    @pl.when(has_right)
    def _():
        halo_copy(1, mt + 1).start()

    def place(w, column):
        column = column.astype(f32)
        for t in range(TF):
            for parity in range(2):
                gpad.at[w, t][pl.ds(8 + parity, H, stride=2), :] = column[t]
        for e in range(3):
            us[e, w, 2:] = gpad[w, :, 7 + e:7 + e + H2, :].astype(bf16)

    for w in range(WD):
        place(w + 1, first[w])

    def b_near_args(c):
        return bsend.at[c], b_near.at[c], bn_sem.at[c], bm_sem.at[c]

    def b_far_args(c):
        return b_pass.at[c], b_far.at[c], bp_sem.at[c], bf_sem.at[c]

    wb_copy.wait()
    for c, cols in enumerate(CHUNKS):
        if c == 1:
            @pl.when(has_right)
            def _():
                halo_copy(0, mt).wait_recv()

            @pl.when(has_left)
            def _():
                halo_copy(1, mt).wait_recv()
            place(0, hrecv[0])
            place(WD + 1, hrecv[1])
        lhs = jnp.concatenate(
            [jnp.concatenate(
                [us[e, (w2 + g + 1) // 2, a:a + TF].reshape(COL, LANES) for w2 in cols], axis=0)
             for a in range(3) for e in range(3) for g in range(3)], axis=1)
        part = jnp.dot(lhs, wb[...].reshape(27 * LANES, wb.shape[2]), preferred_element_type=f32)
        part = part.T.astype(bf16)
        for j in range(chans):
            bsend[c, j] = part[j * ch:(j + 1) * ch]
        for k in order:
            near_copy(k, *b_near_args(c)).start()

    for c in range(2):
        for k in range(1, pairs):
            near_copy(k, *b_near_args(c)).wait_recv()
            own = bsend[c, 2 * lax.rem(pair + k, pairs) + side].astype(f32)
            b_pass[c, k - 1] = (own + b_near[c, k].astype(f32)).astype(bf16)
            far_copy(k, *b_far_args(c)).start()

    bias = jnp.concatenate([bias_b[...]] * 2, axis=1)
    for c, cols in enumerate(CHUNKS):
        near_copy(0, *b_near_args(c)).wait_recv()
        total = bsend[c, mc].astype(f32) + b_near[c, 0].astype(f32) + bias
        for k in range(1, pairs):
            far_copy(k, *b_far_args(c)).wait_recv()
            total = total + b_far[c, k - 1].astype(f32)
        y = silu(total).astype(bf16)
        for i, w2 in enumerate(cols):
            out_ref[w2] = y[:, i * COL:(i + 1) * COL]

    for k in range(1, tiles):
        field_copy(k, mt, lax.rem(mt + k, tiles)).wait_send()
    for near_args, far_args in ((a_near_args, a_far_args),
                                (b_near_args(0), b_far_args(0)), (b_near_args(1), b_far_args(1))):
        for k in range(pairs):
            near_copy(k, *near_args).wait_send()
        for k in range(1, pairs):
            far_copy(k, *far_args).wait_send()

    @pl.when(has_left)
    def _():
        halo_copy(0, mt - 1).wait_send()

    @pl.when(has_right)
    def _():
        halo_copy(1, mt + 1).wait_send()


def local(tokens, conv_a, bias_a, conv_b, bias_b):
    tiles = lax.axis_size("tile")
    chans = lax.axis_size("chan")
    ch = tokens.shape[1]
    pairs = chans // 2
    rows = TF * H // tiles
    full = conv_a.shape[2]
    width = tiles * WD
    f32, bf16 = jnp.float32, jnp.bfloat16
    vm, dma = pltpu.VMEM, pltpu.SemaphoreType.DMA
    out = pl.pallas_call(
        functools.partial(kernel, tiles, chans, ch, rows),
        out_shape=jax.ShapeDtypeStruct((2 * WD, ch, COL), bf16),
        in_specs=[pl.BlockSpec(memory_space=pltpu.HBM)] * 5,
        out_specs=pl.BlockSpec(memory_space=vm),
        scratch_shapes=[
            vm((ch, rows * width), bf16),
            vm((rows * width, LANES), f32),
            vm((width + 2, rows, LANES), bf16),
            vm((tiles, WD + 2, rows, LANES), bf16),
            vm((WD + 2, TF, H + 16, LANES), f32),
            vm((3, WD + 2, TF + 2, H, LANES), bf16),
            vm((27, LANES, full), bf16),
            vm((27, LANES, full), bf16),
            vm((1, ch), f32),
            vm((1, ch), f32),
            vm((ch, LANES), f32),
            vm((ch, LANES), f32),
            vm((chans, ch, POS), f32),
            vm((pairs, ch, POS), f32),
            vm((pairs - 1, ch, POS), f32),
            vm((pairs - 1, ch, POS), f32),
            vm((2, TF, H, LANES), bf16),
            vm((2, TF, H, LANES), bf16),
            vm((WD + 2, TF, H2 + 16, LANES), f32),
            vm((3, WD + 2, TF + 2, H2, LANES), bf16),
            vm((2, chans, ch, 2 * COL), bf16),
            vm((2, pairs, ch, 2 * COL), bf16),
            vm((2, pairs - 1, ch, 2 * COL), bf16),
            vm((2, pairs - 1, ch, 2 * COL), bf16),
            dma((5,)),
            dma((tiles - 1,)),
            dma((tiles - 1,)),
            dma((pairs,)),
            dma((pairs,)),
            dma((pairs - 1,)),
            dma((pairs - 1,)),
            dma((2,)),
            dma((2,)),
            dma((2, pairs)),
            dma((2, pairs)),
            dma((2, pairs - 1)),
            dma((2, pairs - 1)),
        ],
        compiler_params=pltpu.CompilerParams(
            collective_id=0, has_side_effects=True, vmem_limit_bytes=63 << 20),
    )(tokens.T, conv_a, bias_a.reshape(1, -1), conv_b, bias_b.reshape(1, -1))
    return out.transpose(1, 0, 2)


def solution(mesh):
    in_specs = (
        P(("groups", "tile"), "chan"),
        P(None, "chan", None),
        P("chan"),
        P(None, "chan", None),
        P("chan"),
    )
    out_specs = P("chan", "tile", "groups")
    return jax.shard_map(local, mesh=mesh, in_specs=in_specs, out_specs=out_specs, check_vma=False)
```
